256 devices in a mesh: pipe: 16 (over z, core), seq: 4 (over y), batch: 4 (over x).
Axes of the slice: x: 4, y: 4, z: 8, core: 2. Of those that a mesh axis runs over, the one named last changes fastest.
Arguments:
- latent: bfloat16 [32, 32, 2560], P('batch', 'seq'), parts along dimension 0, may hold values from -6 to 6
- w_qkv: bfloat16 [16, 2560, 3, 2560], P('pipe', None, None, 'seq')
- modulation: float32 [16, 8, 3, 2560], P('pipe'), may hold values from -3 to 3
- timestep: int32 [1], replicated, may hold values from 0 to 7
- order: int32 [32], P('batch'), parts along dimension 0, may hold values from 0 to 7, each once
- tiles: int32 [64, 6], P('batch'), parts along dimension 0, may hold values from 0 to 15, as said below
- stale_kv: bfloat16 [16, 32, 32, 2, 2560], P('pipe', 'batch', None, None, 'seq'), parts along dimension 1, may hold values from -6 to 6
Outputs:
- section_out: bfloat16 [16, 32, 32, 2560], P('pipe', 'batch', 'seq'), parts along dimension 1
The draws below stay inside these ranges and needn't reach their ends.
There are 4 independent parts, one for each index of `batch`. The reference program is written for one: setup_inputs(seed, part) draws one part's arguments, and reference() takes and returns one part's arrays. A program takes and returns all parts, laid end to end along the dimension named above; an argument that names none is the same for every part. Nothing has to cross between parts.
Inputs may be any that keep to these rules, and one draw needn't show every extreme that they name: Row g lists tile g first, then 6 - 1 distinct other tiles whose index differs from g modulo 16 by 1 to 5.
All inputs are finite; a program needn't handle non-finite values.
Results may differ from the reference program's by a relative error of at most 0.019.
Values may be sent and summed in bfloat16 or wider, within the bound.
No kernel may reach another device: no remote copies, remote signals or barrier semaphores. Data moves between devices by JAX's collectives and lax.ppermute only.
A program may use at most 128 MiB of HBM per device.

```python
import jax
import jax.numpy as jnp
from jax import lax

D = 2560
HEADS = 20
HEAD_DIM = 128
STEPS = 8
PATCHES = 8
TILES_P = 2
NSEL = 6
SECTIONS = 16
PATCH_TOK = 32
TILE = 16
NTILES = 16


def draw_w_qkv(key, part):
    sampled = jax.random.normal(key, (SECTIONS, D, 3, D), jnp.float32) * D ** (-0.5)
    return sampled.astype(jnp.bfloat16)


def draw_tiles(key, part):
    window = 2 * (NSEL - 1)
    half_window = window // 2
    row_keys = jax.random.split(key, NTILES)
    picked = jax.vmap(lambda subkey: jax.random.permutation(subkey, window))(row_keys)[:, :NSEL - 1]
    offsets = jnp.where(picked < half_window, picked - half_window, picked - half_window + 1)
    anchor_tile = jnp.arange(NTILES, dtype=jnp.int32)[:, None]
    others = (anchor_tile + offsets) % NTILES
    return jnp.concatenate([anchor_tile, others.astype(jnp.int32)], axis=1).astype(jnp.int32)


def block_scale(rng, shape, cuts, smallest, top_value):
    loudness, own = 1.0, jax.random.fold_in(rng, 6)
    for dim, parts in cuts:
        draws = jnp.exp(jax.random.uniform(jax.random.fold_in(own, dim), (parts,), jnp.float32, smallest / len(cuts), top_value / len(cuts)))
        loudness = loudness * jnp.repeat(draws, shape[dim] // parts).reshape([-1 if axis == dim else 1 for axis in range(len(shape))])
    return loudness


def gaussian(stream_key, shape, deviation, limit, cuts=(), kind=jnp.bfloat16):
    drawn = deviation * jax.random.normal(stream_key, shape, jnp.float32)
    if cuts:
        drawn = drawn * block_scale(stream_key, shape, cuts, -0.22, 0.18)
    return jnp.clip(drawn, -limit, limit).astype(kind)


def setup_inputs(seed: int = 0, part: int = 0) -> dict:
    arg_keys = jax.random.split(jax.random.key(seed), 8)
    part_splits = jax.random.split(jax.random.fold_in(arg_keys[7], part), 8)
    return {
        "latent": gaussian(part_splits[0], (PATCHES, PATCH_TOK, D), 1.0, 6.0, ((1, 4),)),
        "w_qkv": draw_w_qkv(jax.random.fold_in(arg_keys[7], 71), part),
        "modulation": gaussian(arg_keys[2], (SECTIONS, STEPS, 3, D), 0.5, 3.0, ((0, 16),), jnp.float32),
        "timestep": jax.random.randint(arg_keys[3], (1,), 0, STEPS).astype(jnp.int32),
        "order": jax.random.permutation(part_splits[4], PATCHES).astype(jnp.int32),
        "tiles": draw_tiles(jax.random.fold_in(jax.random.fold_in(arg_keys[7], part), 71), part),
        "stale_kv": gaussian(part_splits[6], (SECTIONS, PATCHES, PATCH_TOK, 2, D), 1.0, 6.0, ((0, 16), (4, 4))),
    }


epsilon = 1e-06

def normalize(row_block, shift_row, scale_row):
    floated = row_block.astype(jnp.float32)
    average = lax.optimization_barrier(jnp.mean(floated, axis=-1, keepdims=True))
    centred = floated - average
    spread = lax.optimization_barrier(jnp.mean(centred * centred, axis=-1, keepdims=True))
    return (centred * lax.rsqrt(spread + epsilon) * (1.0 + scale_row) + shift_row).astype(jnp.bfloat16)

def attend(query, buffer, chosen_tiles):
    blocks = buffer.reshape(NTILES, TILE, 2, D)
    picked = blocks[chosen_tiles].reshape(TILES_P, NSEL * TILE, 2, HEADS, HEAD_DIM).astype(jnp.float32)
    queries = query.reshape(TILES_P, TILE, HEADS, HEAD_DIM).astype(jnp.float32)
    scores = jnp.einsum('qthd,qkhd->qhtk', queries, picked[:, :, 0]) * HEAD_DIM ** (-0.5)
    probabilities = jax.nn.softmax(scores, axis=-1).astype(jnp.bfloat16)
    mixed = jnp.einsum('qhtk,qkhd->qthd', probabilities.astype(jnp.float32), picked[:, :, 1])
    return mixed.reshape(PATCH_TOK, D).astype(jnp.bfloat16)

def reference(latent, w_qkv, modulation, timestep, order, tiles, stale_kv):
    hidden = latent
    section_outputs = []
    for section_id in range(SECTIONS):
        mod_row = modulation[section_id, timestep[0]]
        buffer = stale_kv[section_id]
        weights = w_qkv[section_id].reshape(D, 3 * D)
        updated = hidden
        for position in range(PATCHES):
            patch_id = order[position].astype(jnp.int32)
            own_rows = hidden[patch_id]
            normed = normalize(own_rows, mod_row[0], mod_row[1])
            projected = jnp.dot(normed, weights, preferred_element_type=jnp.float32).astype(jnp.bfloat16)
            projected = projected.reshape(PATCH_TOK, 3, D)
            buffer = buffer.at[patch_id].set(projected[:, 1:])
            chosen = lax.dynamic_slice_in_dim(tiles, (patch_id * TILES_P).astype(jnp.int32), TILES_P, 0)
            attended = attend(projected[:, 0], buffer, chosen)
            result = (own_rows.astype(jnp.float32) + mod_row[2] * attended.astype(jnp.float32)).astype(jnp.bfloat16)
            updated = updated.at[patch_id].set(result)
        hidden = updated
        section_outputs.append(hidden)
    return jnp.stack(section_outputs)
```

```python
import jax
import jax.numpy as jnp
from jax import lax
from jax.experimental import pallas as pl
from jax.experimental.pallas import tpu as pltpu
from jax.sharding import PartitionSpec as P

HEAD_DIM = 128
TILES_P = 2
epsilon = 1e-06
MASKED = -3.0e38


def layer_kernel(
    scalars,
    piece0,
    piece1,
    piece2,
    piece3,
    latent,
    weights,
    stale_k,
    stale_v,
    codes,
    mods,
    out_before,
    out,
    w_buf,
    piece_buf,
    normed,
    projected,
    k_buf,
    v_buf,
    code_buf,
    mod_buf,
    out_buf,
    piece_sem,
    w_sem,
    misc_sem,
):
    rows, width = normed.shape
    local_w = piece_buf.shape[2]
    n_cols = w_buf.shape[1]
    step_cols = 512
    pieces = (piece0, piece1, piece2, piece3)
    count = len(pieces)
    w_blocks = [(c, min(step_cols, n_cols - c)) for c in range(0, n_cols, step_cols)]
    seq_rank = scalars[2]

    def source(k):
        return lax.rem(seq_rank + count - k, count)

    @pl.when(scalars[0] == 1)
    def _():
        @pl.when(scalars[1] == 1)
        def _():
            for k in range(count):
                start = pl.multiple_of(source(k) * local_w, 128)
                pltpu.make_async_copy(
                    latent.at[:, pl.ds(start, local_w)], piece_buf.at[k], piece_sem.at[k]
                ).start()

        @pl.when(scalars[1] == 0)
        def _():
            for k in range(count):
                pltpu.make_async_copy(pieces[k], piece_buf.at[k], piece_sem.at[k]).start()

        mod_copy = pltpu.make_async_copy(mods, mod_buf, misc_sem.at[0])
        mod_copy.start()
        w_copies = []
        for b, (c, n) in enumerate(w_blocks):
            copy = pltpu.make_async_copy(
                weights.at[:, pl.ds(c, n)], w_buf.at[:, pl.ds(c, n)], w_sem.at[b]
            )
            copy.start()
            w_copies.append(copy)
        late = [
            pltpu.make_async_copy(a, b, misc_sem.at[1 + i])
            for i, (a, b) in enumerate(((stale_k, k_buf), (stale_v, v_buf), (codes, code_buf)))
        ]
        for copy in late:
            copy.start()
        for k in range(count):
            pltpu.make_async_copy(pieces[k], piece_buf.at[k], piece_sem.at[k]).wait()
        mod_copy.wait()

        shifts = [mod_buf[source(k)] for k in range(count)]
        scales = [1.0 + mod_buf[count + source(k)] for k in range(count)]
        block = 16

        def norm_rows(r, carry):
            at = pl.ds(pl.multiple_of(r * block, block), block)
            parts = [piece_buf[k, at, :].astype(jnp.float32) for k in range(count)]
            total = sum(jnp.sum(part, axis=-1, keepdims=True) for part in parts)
            average = total / width
            parts = [part - average for part in parts]
            squares = sum(jnp.sum(part * part, axis=-1, keepdims=True) for part in parts)
            factor = lax.rsqrt(squares / width + epsilon)
            for k in range(count):
                start = pl.multiple_of(source(k) * local_w, 128)
                normed[at, pl.ds(start, local_w)] = (
                    parts[k] * factor * scales[k] + shifts[k]
                ).astype(jnp.bfloat16)
            return carry

        lax.fori_loop(0, rows // block, norm_rows, 0, unroll=2)

        for b, (c, n) in enumerate(w_blocks):
            w_copies[b].wait()
            projected[:, pl.ds(c, n)] = jnp.dot(
                normed[...], w_buf[:, pl.ds(c, n)], preferred_element_type=jnp.float32
            ).astype(jnp.bfloat16)
        for copy in late:
            copy.wait()

        gate = mod_buf[2 * count + seq_rank]
        q_rows = min(128, rows)
        nt = (((1,), (1,)), ((), ()))
        for head in range(local_w // HEAD_DIM):
            cols = pl.ds(head * HEAD_DIM, HEAD_DIM)
            k_new = projected[:, pl.ds(local_w + head * HEAD_DIM, HEAD_DIM)]
            v_new = projected[:, pl.ds(2 * local_w + head * HEAD_DIM, HEAD_DIM)]
            k_old = k_buf[:, cols]
            v_old = v_buf[:, cols]
            for r in range(0, rows, q_rows):
                at = pl.ds(r, q_rows)
                query = projected[at, cols]
                code = code_buf[at, :]
                fresh = code > 1.5
                new = lax.dot_general(query, k_new, nt, preferred_element_type=jnp.float32)
                old = lax.dot_general(query, k_old, nt, preferred_element_type=jnp.float32)
                scores = jnp.where(fresh, new, old) * HEAD_DIM ** (-0.5)
                scores = jnp.where(code > 0.5, scores, MASKED)
                largest = jnp.max(scores, axis=-1, keepdims=True)
                raised = jnp.exp(scores - largest)
                total = jnp.sum(raised, axis=-1, keepdims=True)
                chances = raised * (1.0 / total)
                of_new = jnp.where(fresh, chances, 0.0).astype(jnp.bfloat16)
                of_old = jnp.where(fresh, 0.0, chances).astype(jnp.bfloat16)
                mixed = jnp.dot(of_new, v_new, preferred_element_type=jnp.float32) + jnp.dot(
                    of_old, v_old, preferred_element_type=jnp.float32
                )
                mixed = mixed.astype(jnp.bfloat16).astype(jnp.float32)
                own = piece_buf[0, at, cols].astype(jnp.float32)
                gate_part = gate[:, head * HEAD_DIM : (head + 1) * HEAD_DIM]
                out_buf[at, cols] = (own + gate_part * mixed).astype(jnp.bfloat16)
        done = pltpu.make_async_copy(out_buf, out, misc_sem.at[4])
        done.start()
        done.wait()


def run_layer(scalars, pieces, latent, weights, stale_k, stale_v, codes, mods, out):
    rows, local_w = out.shape
    width = latent.shape[1]
    any_spec = pl.BlockSpec(memory_space=pl.ANY)
    return pl.pallas_call(
        layer_kernel,
        out_shape=jax.ShapeDtypeStruct(out.shape, out.dtype),
        in_specs=[pl.BlockSpec(memory_space=pltpu.SMEM)] + [any_spec] * 11,
        out_specs=any_spec,
        scratch_shapes=[
            pltpu.VMEM(weights.shape, jnp.bfloat16),
            pltpu.VMEM((4, rows, local_w), jnp.bfloat16),
            pltpu.VMEM((rows, width), jnp.bfloat16),
            pltpu.VMEM((rows, 3 * local_w), jnp.bfloat16),
            pltpu.VMEM(stale_k.shape, jnp.bfloat16),
            pltpu.VMEM(stale_v.shape, jnp.bfloat16),
            pltpu.VMEM(codes.shape, jnp.float32),
            pltpu.VMEM(mods.shape, jnp.float32),
            pltpu.VMEM((rows, local_w), jnp.bfloat16),
            pltpu.SemaphoreType.DMA((4,)),
            pltpu.SemaphoreType.DMA((4,)),
            pltpu.SemaphoreType.DMA((5,)),
        ],
        input_output_aliases={11: 0},
        compiler_params=pltpu.CompilerParams(vmem_limit_bytes=40 * 1024 * 1024),
        name="layer",
    )(scalars, *pieces, latent, weights, stale_k, stale_v, codes, mods, out)


def pair_list(pipe_count, seq_count, parity, by):
    return [
        (s * seq_count + q, (s + 1) * seq_count + (q + by) % seq_count)
        for s in range(parity, pipe_count - 1, 2)
        for q in range(seq_count)
    ]


def key_codes(order, tiles):
    patches = order.shape[0]
    n_tiles = tiles.shape[0]
    ids = jnp.arange(patches, dtype=jnp.int32)
    place = jnp.sum(jnp.where(order[None, :] == ids[:, None], ids[None, :], 0), axis=1)
    place = jnp.repeat(place, n_tiles // patches)
    tile_ids = jnp.arange(n_tiles, dtype=jnp.int32)
    chosen = jnp.any(tiles[:, :, None] == tile_ids[None, None, :], axis=1)
    fresh = place[None, :] <= place[:, None]
    return jnp.where(chosen, jnp.where(fresh, 2.0, 1.0), 0.0).astype(jnp.float32)


def local(latent, w_qkv, modulation, timestep, order, tiles, stale_kv):
    patches, rows_dev, width = latent.shape
    local_w = w_qkv.shape[3]
    seq_count = lax.axis_size("seq")
    pipe_count = lax.axis_size("pipe")
    section_rank = lax.axis_index("pipe")
    seq_rank = lax.axis_index("seq")
    patch_tok = rows_dev * seq_count
    rows = patches * patch_tok
    tile_len = patch_tok // TILES_P
    weights = w_qkv[0].reshape(width, 3 * local_w)
    mod_rows = lax.dynamic_index_in_dim(modulation[0], timestep[0], 0, keepdims=False)
    mods = mod_rows.reshape(3 * seq_count, 1, local_w)
    stale_k = stale_kv[0, :, :, 0].reshape(rows, local_w)
    stale_v = stale_kv[0, :, :, 1].reshape(rows, local_w)
    codes = jnp.repeat(jnp.repeat(key_codes(order, tiles), tile_len, 0), tile_len, 1)

    spread = lax.all_to_all(
        jnp.broadcast_to(latent[None], (seq_count, *latent.shape)), "seq", 0, 0, tiled=True
    )
    tokens = jnp.moveaxis(spread, 0, 1).reshape(rows, width)

    def scalars_at(turn):
        active = (section_rank == turn).astype(jnp.int32)
        first = (section_rank == 0).astype(jnp.int32)
        return jnp.stack([active, first, seq_rank.astype(jnp.int32)])

    def send(out, parity):
        return tuple(
            lax.ppermute(out, ("pipe", "seq"), pair_list(pipe_count, seq_count, parity, by))
            for by in range(seq_count)
        )

    def layer(turn, pieces, out):
        return run_layer(
            scalars_at(turn), pieces, tokens, weights, stale_k, stale_v, codes, mods, out
        )

    def two_turns(carry, i):
        pieces, out = carry
        out = layer(2 * i, pieces, out)
        pieces = send(out, 0)
        out = layer(2 * i + 1, pieces, out)
        pieces = send(out, 1)
        return (pieces, out), None

    empty = jnp.zeros((rows, local_w), jnp.bfloat16)
    (unused, out), _ = lax.scan(
        two_turns,
        ((empty,) * seq_count, empty),
        jnp.arange(pipe_count // 2, dtype=jnp.int32),
    )
    columns = out.reshape(patches, patch_tok, local_w)
    finished = lax.all_to_all(columns, "seq", split_axis=1, concat_axis=2, tiled=True)
    return finished[None]


def solution(mesh):
    return jax.shard_map(
        local,
        mesh=mesh,
        in_specs=(
            P("batch", "seq", None),
            P("pipe", None, None, "seq"),
            P("pipe", None, None, None),
            P(),
            P("batch"),
            P("batch", None),
            P("pipe", "batch", None, None, "seq"),
        ),
        out_specs=P("pipe", "batch", "seq", None),
        check_vma=False,
    )
```

```python
import functools

import jax
import jax.numpy as jnp
from jax import lax
from jax.experimental import pallas as pl
from jax.experimental.pallas import tpu as pltpu
from jax.sharding import PartitionSpec as P

HEAD_DIM = 128
TILES_P = 2
epsilon = 1e-06
MASKED = -3.0e38
CHUNKS = 4
SEND_ORDER = (2, 1, 3, 0)


def layer_kernel(
    parity,
    chunks,
    scalars,
    order,
    piece0,
    piece1,
    piece2,
    piece3,
    latent,
    weights,
    chosen,
    mods,
    kv_before,
    results_before,
    out,
    kv,
    results,
    w_buf,
    piece_buf,
    normed,
    projected,
    kv_buf,
    code_buf,
    mod_buf,
    out_buf,
    piece_sem,
    w_sem,
    misc_sem,
):
    rows, width = normed.shape
    local_w = piece_buf.shape[2]
    all_rows = kv_buf.shape[1]
    pieces = (piece0, piece1, piece2, piece3)
    count = len(pieces)
    patches = order.shape[0]
    per_chunk = patches // chunks
    patch_tok = rows // per_chunk
    w_blocks = [(part, c, n) for part in range(3) for c, n in ((0, 256), (256, 384))]
    section_rank = scalars[1]
    seq_rank = scalars[2]
    age = 2 * scalars[0] + parity - section_rank
    chunk = lax.div(age, 2)
    active = (age >= 0) & (lax.rem(age, 2) == 0) & (chunk < chunks)

    def source(k):
        return lax.rem(seq_rank + count - k, count)

    @pl.when(active)
    def _():
        patch_rows = []
        for i in range(per_chunk):
            patch = order[chunk * per_chunk + i]
            patch_rows.append(pl.ds(pl.multiple_of(patch * patch_tok, patch_tok), patch_tok))

        @pl.when(section_rank == 0)
        def _():
            for k in range(count):
                start = pl.multiple_of(source(k) * local_w, 128)
                for i in range(per_chunk):
                    pltpu.make_async_copy(
                        latent.at[patch_rows[i], pl.ds(start, local_w)],
                        piece_buf.at[k, pl.ds(i * patch_tok, patch_tok)],
                        piece_sem.at[k],
                    ).start()

        @pl.when(section_rank != 0)
        def _():
            for k in range(count):
                pltpu.make_async_copy(pieces[k], piece_buf.at[k], piece_sem.at[k]).start()

        mod_copy = pltpu.make_async_copy(mods, mod_buf, misc_sem.at[0])
        mod_copy.start()
        w_copies = []
        for b, (part, c, n) in enumerate(w_blocks):
            copy = pltpu.make_async_copy(
                weights.at[part, :, pl.ds(c, n)], w_buf.at[part, :, pl.ds(c, n)], w_sem.at[b]
            )
            copy.start()
            w_copies.append(copy)
        late = [pltpu.make_async_copy(kv_before, kv_buf, misc_sem.at[1])]
        for i in range(per_chunk):
            late.append(
                pltpu.make_async_copy(chosen.at[patch_rows[i]], code_buf.at[i], misc_sem.at[2 + i])
            )
        for copy in late:
            copy.start()
        for k in range(count):
            pltpu.make_async_copy(pieces[k], piece_buf.at[k], piece_sem.at[k]).wait()
        mod_copy.wait()

        shifts = [mod_buf[source(k)] for k in range(count)]
        scales = [1.0 + mod_buf[count + source(k)] for k in range(count)]
        block = 16

        def norm_rows(r, carry):
            at = pl.ds(pl.multiple_of(r * block, block), block)
            parts = [piece_buf[k, at, :].astype(jnp.float32) for k in range(count)]
            total = sum(jnp.sum(part, axis=-1, keepdims=True) for part in parts)
            average = total / width
            parts = [part - average for part in parts]
            squares = sum(jnp.sum(part * part, axis=-1, keepdims=True) for part in parts)
            factor = lax.rsqrt(squares / width + epsilon)
            for k in range(count):
                start = pl.multiple_of(source(k) * local_w, 128)
                normed[at, pl.ds(start, local_w)] = (
                    parts[k] * factor * scales[k] + shifts[k]
                ).astype(jnp.bfloat16)
            return carry

        lax.fori_loop(0, rows // block, norm_rows, 0, unroll=2)

        for b, (part, c, n) in enumerate(w_blocks):
            w_copies[b].wait()
            projected[part, :, pl.ds(c, n)] = jnp.dot(
                normed[...], w_buf[part, :, pl.ds(c, n)], preferred_element_type=jnp.float32
            ).astype(jnp.bfloat16)
        for copy in late:
            copy.wait()

        gate = mod_buf[2 * count + seq_rank]
        nt = (((1,), (1,)), ((), ()))
        backs = []
        for i in range(per_chunk):
            at = pl.ds(i * patch_tok, patch_tok)
            for part in range(2):
                kv_buf[part, patch_rows[i], :] = projected[1 + part, at, :]
                backs.append(
                    pltpu.make_async_copy(
                        projected.at[1 + part, at],
                        kv.at[part, patch_rows[i]],
                        misc_sem.at[2 + 2 * per_chunk + 2 * i + part],
                    )
                )
                backs[-1].start()
            attended = code_buf[i] > 0.5
            for head in range(local_w // HEAD_DIM):
                cols = pl.ds(head * HEAD_DIM, HEAD_DIM)
                scores = lax.dot_general(
                    projected[0, at, cols],
                    kv_buf[0, :, cols],
                    nt,
                    preferred_element_type=jnp.float32,
                )
                scores = jnp.where(attended, scores * HEAD_DIM ** (-0.5), MASKED)
                largest = jnp.max(scores, axis=-1, keepdims=True)
                raised = jnp.exp(scores - largest)
                total = jnp.sum(raised, axis=-1, keepdims=True)
                chances = (raised * (1.0 / total)).astype(jnp.bfloat16)
                mixed = jnp.dot(chances, kv_buf[1, :, cols], preferred_element_type=jnp.float32)
                mixed = mixed.astype(jnp.bfloat16).astype(jnp.float32)
                own = piece_buf[0, at, cols].astype(jnp.float32)
                gate_part = gate[:, head * HEAD_DIM : (head + 1) * HEAD_DIM]
                out_buf[at, cols] = (own + gate_part * mixed).astype(jnp.bfloat16)
        backs.append(pltpu.make_async_copy(out_buf, out, misc_sem.at[1]))
        backs[-1].start()
        for i in range(per_chunk):
            backs.append(
                pltpu.make_async_copy(
                    out_buf.at[pl.ds(i * patch_tok, patch_tok)],
                    results.at[patch_rows[i]],
                    misc_sem.at[2 + per_chunk + i],
                )
            )
            backs[-1].start()
        for copy in backs:
            copy.wait()


def run_layer(parity, chunks, scalars, order, pieces, latent, weights, chosen, mods, kv, results):
    rows, local_w = pieces[0].shape
    width = latent.shape[1]
    per_chunk = order.shape[0] // chunks
    any_spec = pl.BlockSpec(memory_space=pl.ANY)
    smem_spec = pl.BlockSpec(memory_space=pltpu.SMEM)
    return pl.pallas_call(
        functools.partial(layer_kernel, parity, chunks),
        out_shape=(
            jax.ShapeDtypeStruct((rows, local_w), jnp.bfloat16),
            jax.ShapeDtypeStruct(kv.shape, kv.dtype),
            jax.ShapeDtypeStruct(results.shape, results.dtype),
        ),
        in_specs=[smem_spec] * 2 + [any_spec] * 10,
        out_specs=(any_spec,) * 3,
        scratch_shapes=[
            pltpu.VMEM(weights.shape, jnp.bfloat16),
            pltpu.VMEM((4, rows, local_w), jnp.bfloat16),
            pltpu.VMEM((rows, width), jnp.bfloat16),
            pltpu.VMEM((3, rows, local_w), jnp.bfloat16),
            pltpu.VMEM(kv.shape, jnp.bfloat16),
            pltpu.VMEM((per_chunk, rows // per_chunk, chosen.shape[1]), jnp.float32),
            pltpu.VMEM(mods.shape, jnp.float32),
            pltpu.VMEM((rows, local_w), jnp.bfloat16),
            pltpu.SemaphoreType.DMA((4,)),
            pltpu.SemaphoreType.DMA((6,)),
            pltpu.SemaphoreType.DMA((2 + 4 * per_chunk,)),
        ],
        input_output_aliases={10: 1, 11: 2},
        compiler_params=pltpu.CompilerParams(vmem_limit_bytes=40 * 1024 * 1024),
        name="layer",
    )(scalars, order, *pieces, latent, weights, chosen, mods, kv, results)


def pair_list(pipe_count, seq_count, parity, by):
    return [
        (s * seq_count + q, (s + 1) * seq_count + (q + by) % seq_count)
        for s in range(parity, pipe_count - 1, 2)
        for q in range(seq_count)
    ]


def chosen_keys(tiles, tile_len):
    n_tiles = tiles.shape[0]
    tile_ids = jnp.arange(n_tiles, dtype=jnp.int32)
    chosen = jnp.any(tiles[:, :, None] == tile_ids[None, None, :], axis=1).astype(jnp.float32)
    return jnp.repeat(jnp.repeat(chosen, tile_len, 0), tile_len, 1)


def local(latent, w_qkv, modulation, timestep, order, tiles, stale_kv):
    patches, rows_dev, width = latent.shape
    local_w = w_qkv.shape[3]
    seq_count = lax.axis_size("seq")
    pipe_count = lax.axis_size("pipe")
    section_rank = lax.axis_index("pipe").astype(jnp.int32)
    seq_rank = lax.axis_index("seq").astype(jnp.int32)
    patch_tok = rows_dev * seq_count
    rows = patches * patch_tok
    chunk_rows = rows // CHUNKS
    weights = jnp.transpose(w_qkv[0], (1, 0, 2))
    mod_rows = lax.dynamic_index_in_dim(modulation[0], timestep[0], 0, keepdims=False)
    mods = mod_rows.reshape(3 * seq_count, 1, local_w)
    kv = jnp.moveaxis(stale_kv[0], 2, 0).reshape(2, rows, local_w)
    chosen = chosen_keys(tiles, patch_tok // TILES_P)

    spread = lax.all_to_all(
        jnp.broadcast_to(latent[None], (seq_count, *latent.shape)), "seq", 0, 0, tiled=True
    )
    tokens = jnp.moveaxis(spread, 0, 1).reshape(rows, width)

    def send(out, parity):
        arrived = [None] * seq_count
        for by in SEND_ORDER:
            arrived[by] = lax.ppermute(
                out, ("pipe", "seq"), pair_list(pipe_count, seq_count, parity, by)
            )
        return tuple(arrived)

    def two_turns(i, carry):
        pieces, kv, results = carry
        scalars = jnp.stack([i, section_rank, seq_rank])
        for parity in range(2):
            out, kv, results = run_layer(
                parity, CHUNKS, scalars, order, pieces, tokens, weights, chosen, mods, kv, results
            )
            pieces = send(out, parity)
        return pieces, kv, results

    empty = jnp.zeros((chunk_rows, local_w), jnp.bfloat16)
    turns = pipe_count + 2 * (CHUNKS - 1)
    unused, kv, results = lax.fori_loop(
        0,
        (turns + 1) // 2,
        two_turns,
        ((empty,) * seq_count, kv, jnp.zeros((rows, local_w), jnp.bfloat16)),
    )
    columns = results.reshape(patches, patch_tok, local_w)
    finished = lax.all_to_all(columns, "seq", split_axis=1, concat_axis=2, tiled=True)
    return finished[None]


def solution(mesh):
    return jax.shard_map(
        local,
        mesh=mesh,
        in_specs=(
            P("batch", "seq", None),
            P("pipe", None, None, "seq"),
            P("pipe", None, None, None),
            P(),
            P("batch"),
            P("batch", None),
            P("pipe", "batch", None, None, "seq"),
        ),
        out_specs=P("pipe", "batch", "seq", None),
        check_vma=False,
    )
```

```python
import functools

import jax
import jax.numpy as jnp
from jax import lax
from jax.experimental import pallas as pl
from jax.experimental.pallas import tpu as pltpu
from jax.sharding import PartitionSpec as P

HEAD_DIM = 128
TILES_P = 2
epsilon = 1e-06
MASKED = -3.0e38
CHUNKS = 4
SEND_ORDER = (2, 1, 3, 0)


def layer_kernel(
    parity,
    chunks,
    scalars,
    order,
    piece0,
    piece1,
    piece2,
    piece3,
    latent,
    weights,
    chosen,
    mods,
    kv_before,
    results_before,
    out,
    kv,
    results,
    w_buf,
    piece_buf,
    normed,
    projected,
    kv_buf,
    code_buf,
    mod_buf,
    out_buf,
    piece_sem,
    w_sem,
    misc_sem,
):
    rows, width = normed.shape
    local_w = piece_buf.shape[2]
    pieces = (piece0, piece1, piece2, piece3)
    count = len(pieces)
    patches = order.shape[0]
    per_chunk = patches // chunks
    patch_tok = rows // per_chunk
    w_blocks = [(part, c, n) for part in range(3) for c, n in ((0, 256), (256, 384))]
    section_rank = scalars[1]
    seq_rank = scalars[2]
    age = 2 * scalars[0] + parity - section_rank
    chunk = lax.div(age, 2)
    active = (age >= 0) & (lax.rem(age, 2) == 0) & (chunk < chunks)

    def source(k):
        return lax.rem(seq_rank + count - k, count)

    @pl.when(active)
    def _():
        patch_rows = []
        for i in range(per_chunk):
            patch = order[chunk * per_chunk + i]
            patch_rows.append(pl.ds(pl.multiple_of(patch * patch_tok, patch_tok), patch_tok))

        @pl.when(section_rank == 0)
        def _():
            for k in range(count):
                start = pl.multiple_of(source(k) * local_w, 128)
                for i in range(per_chunk):
                    pltpu.make_async_copy(
                        latent.at[patch_rows[i], pl.ds(start, local_w)],
                        piece_buf.at[k, pl.ds(i * patch_tok, patch_tok)],
                        piece_sem.at[k],
                    ).start()

        @pl.when(section_rank != 0)
        def _():
            for k in range(count):
                pltpu.make_async_copy(pieces[k], piece_buf.at[k], piece_sem.at[k]).start()

        mod_copy = pltpu.make_async_copy(mods, mod_buf, misc_sem.at[0])
        mod_copy.start()
        w_copies = []
        for b, (part, c, n) in enumerate(w_blocks):
            copy = pltpu.make_async_copy(
                weights.at[part, :, pl.ds(c, n)], w_buf.at[part, :, pl.ds(c, n)], w_sem.at[b]
            )
            copy.start()
            w_copies.append(copy)
        late = []
        for i in range(per_chunk):
            late.append(
                pltpu.make_async_copy(
                    kv_before, kv_buf.at[i], misc_sem.at[2 + 4 * per_chunk + i]
                )
            )
            late.append(
                pltpu.make_async_copy(chosen.at[patch_rows[i]], code_buf.at[i], misc_sem.at[2 + i])
            )
        for copy in late:
            copy.start()
        for k in range(count):
            pltpu.make_async_copy(pieces[k], piece_buf.at[k], piece_sem.at[k]).wait()
        mod_copy.wait()

        shifts = [mod_buf[source(k)] for k in range(count)]
        scales = [1.0 + mod_buf[count + source(k)] for k in range(count)]
        block = 16

        def norm_rows(r, carry):
            at = pl.ds(pl.multiple_of(r * block, block), block)
            parts = [piece_buf[k, at, :].astype(jnp.float32) for k in range(count)]
            total = sum(jnp.sum(part, axis=-1, keepdims=True) for part in parts)
            average = total / width
            parts = [part - average for part in parts]
            squares = sum(jnp.sum(part * part, axis=-1, keepdims=True) for part in parts)
            factor = lax.rsqrt(squares / width + epsilon)
            for k in range(count):
                start = pl.multiple_of(source(k) * local_w, 128)
                normed[at, pl.ds(start, local_w)] = (
                    parts[k] * factor * scales[k] + shifts[k]
                ).astype(jnp.bfloat16)
            return carry

        lax.fori_loop(0, rows // block, norm_rows, 0, unroll=2)

        for b, (part, c, n) in enumerate(w_blocks):
            w_copies[b].wait()
            projected[part, :, pl.ds(c, n)] = jnp.dot(
                normed[...], w_buf[part, :, pl.ds(c, n)], preferred_element_type=jnp.float32
            ).astype(jnp.bfloat16)
        for copy in late:
            copy.wait()

        gate = mod_buf[2 * count + seq_rank]
        nt = (((1,), (1,)), ((), ()))
        heads = local_w // HEAD_DIM
        chunk_at = [pl.ds(i * patch_tok, patch_tok) for i in range(per_chunk)]
        head_at = [pl.ds(head * HEAD_DIM, HEAD_DIM) for head in range(heads)]
        backs = []
        chances = []
        for i in range(per_chunk):
            for j in range(i + 1):
                for part in range(2):
                    kv_buf[i, part, patch_rows[j], :] = projected[1 + part, chunk_at[j], :]
        for i in range(per_chunk):
            for part in range(2):
                backs.append(
                    pltpu.make_async_copy(
                        projected.at[1 + part, chunk_at[i]],
                        kv.at[part, patch_rows[i]],
                        misc_sem.at[2 + 2 * per_chunk + 2 * i + part],
                    )
                )
                backs[-1].start()
            scores = jnp.concatenate(
                [
                    lax.dot_general(
                        projected[0, chunk_at[i], cols],
                        kv_buf[i, 0, :, cols],
                        nt,
                        preferred_element_type=jnp.float32,
                    )
                    for cols in head_at
                ],
                axis=0,
            )
            attended = jnp.concatenate([code_buf[i] > 0.5] * heads, axis=0)
            scores = jnp.where(attended, scores * HEAD_DIM ** (-0.5), MASKED)
            largest = jnp.max(scores, axis=-1, keepdims=True)
            raised = jnp.exp(scores - largest)
            total = jnp.sum(raised, axis=-1, keepdims=True)
            chances.append((raised * (1.0 / total)).astype(jnp.bfloat16))
        for i in range(per_chunk):
            for head, cols in enumerate(head_at):
                mixed = jnp.dot(
                    chances[i][head * patch_tok : (head + 1) * patch_tok],
                    kv_buf[i, 1, :, cols],
                    preferred_element_type=jnp.float32,
                )
                mixed = mixed.astype(jnp.bfloat16).astype(jnp.float32)
                own = piece_buf[0, chunk_at[i], cols].astype(jnp.float32)
                gate_part = gate[:, head * HEAD_DIM : (head + 1) * HEAD_DIM]
                out_buf[chunk_at[i], cols] = (own + gate_part * mixed).astype(jnp.bfloat16)
        backs.append(pltpu.make_async_copy(out_buf, out, misc_sem.at[1]))
        backs[-1].start()
        for i in range(per_chunk):
            backs.append(
                pltpu.make_async_copy(
                    out_buf.at[pl.ds(i * patch_tok, patch_tok)],
                    results.at[patch_rows[i]],
                    misc_sem.at[2 + per_chunk + i],
                )
            )
            backs[-1].start()
        for copy in backs:
            copy.wait()


def keep_in_vmem(parity, scalars, value, after):
    def body(scalars, src, after, dst, sem):
        @pl.when(lax.rem(scalars[1], 2) == parity)
        def _():
            copy = pltpu.make_async_copy(src, dst, sem)
            copy.start()
            copy.wait()

    any_spec = pl.BlockSpec(memory_space=pl.ANY)
    return pl.pallas_call(
        body,
        out_shape=pltpu.VMEM(value.shape, value.dtype),
        in_specs=[pl.BlockSpec(memory_space=pltpu.SMEM), any_spec, any_spec],
        out_specs=any_spec,
        scratch_shapes=[pltpu.SemaphoreType.DMA(())],
        compiler_params=pltpu.CompilerParams(vmem_limit_bytes=1024 * 1024),
        name="keep",
    )(scalars, value, after)


def run_layer(parity, chunks, scalars, order, pieces, latent, weights, chosen, mods, kv, results):
    rows, local_w = pieces[0].shape
    width = latent.shape[1]
    per_chunk = order.shape[0] // chunks
    any_spec = pl.BlockSpec(memory_space=pl.ANY)
    smem_spec = pl.BlockSpec(memory_space=pltpu.SMEM)
    return pl.pallas_call(
        functools.partial(layer_kernel, parity, chunks),
        out_shape=(
            jax.ShapeDtypeStruct((rows, local_w), jnp.bfloat16),
            jax.ShapeDtypeStruct(kv.shape, kv.dtype),
            jax.ShapeDtypeStruct(results.shape, results.dtype),
        ),
        in_specs=[smem_spec] * 2 + [any_spec] * 10,
        out_specs=(any_spec,) * 3,
        scratch_shapes=[
            pltpu.VMEM(weights.shape, jnp.bfloat16),
            pltpu.VMEM((4, rows, local_w), jnp.bfloat16),
            pltpu.VMEM((rows, width), jnp.bfloat16),
            pltpu.VMEM((3, rows, local_w), jnp.bfloat16),
            pltpu.VMEM((per_chunk, *kv.shape), jnp.bfloat16),
            pltpu.VMEM((per_chunk, rows // per_chunk, chosen.shape[1]), jnp.float32),
            pltpu.VMEM(mods.shape, jnp.float32),
            pltpu.VMEM((rows, local_w), jnp.bfloat16),
            pltpu.SemaphoreType.DMA((4,)),
            pltpu.SemaphoreType.DMA((6,)),
            pltpu.SemaphoreType.DMA((2 + 5 * per_chunk,)),
        ],
        input_output_aliases={10: 1, 11: 2},
        compiler_params=pltpu.CompilerParams(vmem_limit_bytes=24 * 1024 * 1024),
        name="layer",
    )(scalars, order, *pieces, latent, weights, chosen, mods, kv, results)


def pair_list(pipe_count, seq_count, parity, by):
    return [
        (s * seq_count + q, (s + 1) * seq_count + (q + by) % seq_count)
        for s in range(parity, pipe_count - 1, 2)
        for q in range(seq_count)
    ]


def chosen_keys(tiles, tile_len):
    n_tiles = tiles.shape[0]
    tile_ids = jnp.arange(n_tiles, dtype=jnp.int32)
    chosen = jnp.any(tiles[:, :, None] == tile_ids[None, None, :], axis=1).astype(jnp.float32)
    return jnp.repeat(jnp.repeat(chosen, tile_len, 0), tile_len, 1)


def local(latent, w_qkv, modulation, timestep, order, tiles, stale_kv):
    patches, rows_dev, width = latent.shape
    local_w = w_qkv.shape[3]
    seq_count = lax.axis_size("seq")
    pipe_count = lax.axis_size("pipe")
    section_rank = lax.axis_index("pipe").astype(jnp.int32)
    seq_rank = lax.axis_index("seq").astype(jnp.int32)
    patch_tok = rows_dev * seq_count
    rows = patches * patch_tok
    chunk_rows = rows // CHUNKS
    weights = jnp.transpose(w_qkv[0], (1, 0, 2))
    mod_rows = lax.dynamic_index_in_dim(modulation[0], timestep[0], 0, keepdims=False)
    mods = mod_rows.reshape(3 * seq_count, 1, local_w)
    kv = jnp.moveaxis(stale_kv[0], 2, 0).reshape(2, rows, local_w)
    chosen = chosen_keys(tiles, patch_tok // TILES_P)

    spread = lax.all_to_all(
        jnp.broadcast_to(latent[None], (seq_count, *latent.shape)), "seq", 0, 0, tiled=True
    )
    tokens = jnp.moveaxis(spread, 0, 1).reshape(rows, width)

    def send(out, parity):
        arrived = [None] * seq_count
        for by in SEND_ORDER:
            arrived[by] = lax.ppermute(
                out, ("pipe", "seq"), pair_list(pipe_count, seq_count, parity, by)
            )
        return tuple(arrived)

    def two_turns(i, carry):
        out, kv, results = carry
        scalars = jnp.stack([i, section_rank, seq_rank])
        for parity in range(2):
            pieces = send(out, 1 - parity)
            held = keep_in_vmem(parity, scalars, weights, out)
            out, kv, results = run_layer(
                parity, CHUNKS, scalars, order, pieces, tokens, held, chosen, mods, kv, results
            )
        return out, kv, results

    turns = pipe_count + 2 * (CHUNKS - 1)
    unused, kv, results = lax.fori_loop(
        0,
        (turns + 1) // 2,
        two_turns,
        (
            jnp.zeros((chunk_rows, local_w), jnp.bfloat16),
            kv,
            jnp.zeros((rows, local_w), jnp.bfloat16),
        ),
    )
    columns = results.reshape(patches, patch_tok, local_w)
    finished = lax.all_to_all(columns, "seq", split_axis=1, concat_axis=2, tiled=True)
    return finished[None]


def solution(mesh):
    return jax.shard_map(
        local,
        mesh=mesh,
        in_specs=(
            P("batch", "seq", None),
            P("pipe", None, None, "seq"),
            P("pipe", None, None, None),
            P(),
            P("batch"),
            P("batch", None),
            P("pipe", "batch", None, None, "seq"),
        ),
        out_specs=P("pipe", "batch", "seq", None),
        check_vma=False,
    )
```

```python
import functools

import jax
import jax.numpy as jnp
from jax import lax
from jax.experimental import pallas as pl
from jax.experimental.pallas import tpu as pltpu
from jax.sharding import PartitionSpec as P


HEAD_DIM = 128
TILES_P = 2
epsilon = 1e-06
MASKED = -3.0e38
CHUNKS = 4
SEND_ORDER = (2, 1, 3, 0)


def attend_kernel(
    parity,
    chunks,
    scalars,
    order,
    fresh,
    own_rows,
    chosen,
    gate_row,
    kv_before,
    results_before,
    out,
    kv,
    results,
    projected,
    own_buf,
    kv_buf,
    code_buf,
    gate_buf,
    out_buf,
    misc_sem,
):
    rows, local_w = own_buf.shape
    per_chunk = order.shape[0] // chunks
    patch_tok = rows // per_chunk
    age = 2 * scalars[0] + parity - scalars[1]
    chunk = lax.div(age, 2)
    active = (age >= 0) & (lax.rem(age, 2) == 0) & (chunk < chunks)

    @pl.when(active)
    def _():
        patch_rows = []
        for i in range(per_chunk):
            patch = order[chunk * per_chunk + i]
            patch_rows.append(pl.ds(pl.multiple_of(patch * patch_tok, patch_tok), patch_tok))
        loads = [
            pltpu.make_async_copy(fresh, projected, misc_sem.at[0]),
            pltpu.make_async_copy(own_rows, own_buf, misc_sem.at[1]),
            pltpu.make_async_copy(gate_row, gate_buf, misc_sem.at[2]),
        ]
        for i in range(per_chunk):
            loads.append(pltpu.make_async_copy(kv_before, kv_buf.at[i], misc_sem.at[3 + i]))
            loads.append(
                pltpu.make_async_copy(
                    chosen.at[patch_rows[i]], code_buf.at[i], misc_sem.at[3 + per_chunk + i]
                )
            )
        for copy in loads:
            copy.start()
        for copy in loads:
            copy.wait()

        gate = gate_buf[...]
        nt = (((1,), (1,)), ((), ()))
        heads = local_w // HEAD_DIM
        chunk_at = [pl.ds(i * patch_tok, patch_tok) for i in range(per_chunk)]
        head_at = [pl.ds(head * HEAD_DIM, HEAD_DIM) for head in range(heads)]
        backs = []
        chances = []
        for i in range(per_chunk):
            for j in range(i + 1):
                for part in range(2):
                    kv_buf[i, part, patch_rows[j], :] = projected[1 + part, chunk_at[j], :]
        for i in range(per_chunk):
            for part in range(2):
                backs.append(
                    pltpu.make_async_copy(
                        projected.at[1 + part, chunk_at[i]],
                        kv.at[part, patch_rows[i]],
                        misc_sem.at[3 + 2 * per_chunk + 2 * i + part],
                    )
                )
                backs[-1].start()
            scores = jnp.concatenate(
                [
                    lax.dot_general(
                        projected[0, chunk_at[i], cols],
                        kv_buf[i, 0, :, cols],
                        nt,
                        preferred_element_type=jnp.float32,
                    )
                    for cols in head_at
                ],
                axis=0,
            )
            attended = jnp.concatenate([code_buf[i] > 0.5] * heads, axis=0)
            scores = jnp.where(attended, scores * HEAD_DIM ** (-0.5), MASKED)
            largest = jnp.max(scores, axis=-1, keepdims=True)
            raised = jnp.exp(scores - largest)
            total = jnp.sum(raised, axis=-1, keepdims=True)
            chances.append((raised * (1.0 / total)).astype(jnp.bfloat16))
        for i in range(per_chunk):
            for head, cols in enumerate(head_at):
                mixed = jnp.dot(
                    chances[i][head * patch_tok : (head + 1) * patch_tok],
                    kv_buf[i, 1, :, cols],
                    preferred_element_type=jnp.float32,
                )
                mixed = mixed.astype(jnp.bfloat16).astype(jnp.float32)
                own = own_buf[chunk_at[i], cols].astype(jnp.float32)
                gate_part = gate[:, head * HEAD_DIM : (head + 1) * HEAD_DIM]
                out_buf[chunk_at[i], cols] = (own + gate_part * mixed).astype(jnp.bfloat16)
        backs.append(pltpu.make_async_copy(out_buf, out, misc_sem.at[0]))
        backs[-1].start()
        for i in range(per_chunk):
            backs.append(
                pltpu.make_async_copy(
                    out_buf.at[pl.ds(i * patch_tok, patch_tok)],
                    results.at[patch_rows[i]],
                    misc_sem.at[3 + i],
                )
            )
            backs[-1].start()
        for copy in backs:
            copy.wait()


def keep_in_vmem(parity, scalars, value, after):
    def body(scalars, src, after, dst, sem):
        @pl.when(lax.rem(scalars[1], 2) == parity)
        def _():
            copy = pltpu.make_async_copy(src, dst, sem)
            copy.start()
            copy.wait()

    any_spec = pl.BlockSpec(memory_space=pl.ANY)
    return pl.pallas_call(
        body,
        out_shape=pltpu.VMEM(value.shape, value.dtype),
        in_specs=[pl.BlockSpec(memory_space=pltpu.SMEM), any_spec, any_spec],
        out_specs=any_spec,
        scratch_shapes=[pltpu.SemaphoreType.DMA(())],
        compiler_params=pltpu.CompilerParams(vmem_limit_bytes=1024 * 1024),
        name="keep",
    )(scalars, value, after)


def run_attend(parity, chunks, scalars, order, fresh, own, chosen, gate, kv, results):
    per_chunk = order.shape[0] // chunks
    any_spec = pl.BlockSpec(memory_space=pl.ANY)
    smem_spec = pl.BlockSpec(memory_space=pltpu.SMEM)
    return pl.pallas_call(
        functools.partial(attend_kernel, parity, chunks),
        out_shape=(
            jax.ShapeDtypeStruct(own.shape, jnp.bfloat16),
            jax.ShapeDtypeStruct(kv.shape, kv.dtype),
            jax.ShapeDtypeStruct(results.shape, results.dtype),
        ),
        in_specs=[smem_spec] * 2 + [any_spec] * 6,
        out_specs=(any_spec,) * 3,
        scratch_shapes=[
            pltpu.VMEM(fresh.shape, jnp.bfloat16),
            pltpu.VMEM(own.shape, jnp.bfloat16),
            pltpu.VMEM((per_chunk, *kv.shape), jnp.bfloat16),
            pltpu.VMEM((per_chunk, own.shape[0] // per_chunk, chosen.shape[1]), jnp.float32),
            pltpu.VMEM(gate.shape, jnp.float32),
            pltpu.VMEM(own.shape, jnp.bfloat16),
            pltpu.SemaphoreType.DMA((3 + 4 * per_chunk,)),
        ],
        input_output_aliases={6: 1, 7: 2},
        compiler_params=pltpu.CompilerParams(vmem_limit_bytes=12 * 1024 * 1024),
        name="attend",
    )(scalars, order, fresh, own, chosen, gate, kv, results)


def normalize(rows, shift_row, scale_row):
    floated = rows.astype(jnp.float32)
    average = jnp.mean(floated, axis=-1, keepdims=True)
    centred = floated - average
    spread = jnp.mean(centred * centred, axis=-1, keepdims=True)
    return (centred * lax.rsqrt(spread + epsilon) * (1.0 + scale_row) + shift_row).astype(
        jnp.bfloat16
    )


def pair_list(pipe_count, seq_count, parity, by):
    return [
        (s * seq_count + q, (s + 1) * seq_count + (q + by) % seq_count)
        for s in range(parity, pipe_count - 1, 2)
        for q in range(seq_count)
    ]


def chosen_keys(tiles, tile_len):
    n_tiles = tiles.shape[0]
    tile_ids = jnp.arange(n_tiles, dtype=jnp.int32)
    chosen = jnp.any(tiles[:, :, None] == tile_ids[None, None, :], axis=1).astype(jnp.float32)
    return jnp.repeat(jnp.repeat(chosen, tile_len, 0), tile_len, 1)


def local(latent, w_qkv, modulation, timestep, order, tiles, stale_kv):
    patches, rows_dev, width = latent.shape
    local_w = w_qkv.shape[3]
    seq_count = lax.axis_size("seq")
    pipe_count = lax.axis_size("pipe")
    section_rank = lax.axis_index("pipe").astype(jnp.int32)
    seq_rank = lax.axis_index("seq").astype(jnp.int32)
    patch_tok = rows_dev * seq_count
    rows = patches * patch_tok
    chunk_rows = rows // CHUNKS
    weights = jnp.transpose(w_qkv[0], (1, 0, 2))
    mod_rows = lax.dynamic_index_in_dim(modulation[0], timestep[0], 0, keepdims=False)
    gate = lax.dynamic_slice_in_dim(mod_rows[2:], seq_rank * local_w, local_w, 1)
    kv = jnp.moveaxis(stale_kv[0], 2, 0).reshape(2, rows, local_w)
    chosen = chosen_keys(tiles, patch_tok // TILES_P)

    quarters = [latent] + [
        lax.ppermute(
            latent, ("pipe", "seq"), [(q, (q + by) % seq_count) for q in range(seq_count)]
        )
        for by in range(1, seq_count)
    ]
    tokens = jnp.stack(
        [lax.select_n((seq_rank + seq_count - j) % seq_count, *quarters) for j in range(seq_count)],
        axis=1,
    ).reshape(patches, patch_tok, width)[order]
    tokens = tokens.reshape(CHUNKS, chunk_rows, width)

    def send(out, parity):
        arrived = [None] * seq_count
        for by in SEND_ORDER:
            arrived[by] = lax.ppermute(
                out, ("pipe", "seq"), pair_list(pipe_count, seq_count, parity, by)
            )
        return tuple(arrived)

    def two_turns(i, carry):
        out, kv, results = carry
        scalars = jnp.stack([i, section_rank, seq_rank])
        for parity in range(2):
            pieces = send(out, 1 - parity)
            held = keep_in_vmem(parity, scalars, weights, out)
            whole = jnp.concatenate(
                [lax.select_n((seq_rank + seq_count - j) % seq_count, *pieces) for j in range(seq_count)],
                axis=1,
            )
            own = pieces[0]
            if parity == 0:
                chunk = jnp.clip(i, 0, CHUNKS - 1)
                entry = lax.dynamic_index_in_dim(tokens, chunk, 0, keepdims=False)
                whole = jnp.where(section_rank == 0, entry, whole)
                entry = lax.dynamic_slice(
                    tokens, (chunk, 0, seq_rank * local_w), (1, chunk_rows, local_w)
                )[0]
                own = jnp.where(section_rank == 0, entry, own)
            normed = normalize(whole, mod_rows[0], mod_rows[1])
            fresh = lax.dot_general(
                normed, held, (((1,), (1,)), ((), ())), preferred_element_type=jnp.float32
            ).astype(jnp.bfloat16)
            fresh = jnp.moveaxis(fresh, 1, 0)
            out, kv, results = run_attend(
                parity, CHUNKS, scalars, order, fresh, own, chosen, gate, kv, results
            )
        return out, kv, results

    turns = pipe_count + 2 * (CHUNKS - 1)
    _, kv, results = lax.fori_loop(
        0,
        (turns + 1) // 2,
        two_turns,
        (
            jnp.zeros((chunk_rows, local_w), jnp.bfloat16),
            kv,
            jnp.zeros((rows, local_w), jnp.bfloat16),
        ),
    )
    columns = results.reshape(patches, patch_tok, local_w)
    finished = lax.all_to_all(columns, "seq", split_axis=1, concat_axis=2, tiled=True)
    return finished[None]


def solution(mesh):
    return jax.shard_map(
        local,
        mesh=mesh,
        in_specs=(
            P("batch", "seq", None),
            P("pipe", None, None, "seq"),
            P("pipe", None, None, None),
            P(),
            P("batch"),
            P("batch", None),
            P("pipe", "batch", None, None, "seq"),
        ),
        out_specs=P("pipe", "batch", "seq", None),
        check_vma=False,
    )
```

```python
import functools

import jax
import jax.numpy as jnp
from jax import lax
from jax.experimental import pallas as pl
from jax.experimental.pallas import tpu as pltpu
from jax.sharding import PartitionSpec as P


HEAD_DIM = 128
TILES_P = 2
epsilon = 1e-06
MASKED = -3.0e38
CHUNKS = 4
SEND_ORDER = (2, 1, 3, 0)


def attend_kernel(
    parity,
    chunks,
    scalars,
    order,
    fresh,
    own_rows,
    chosen,
    gate_row,
    kv_before,
    results_before,
    out,
    kv,
    results,
    projected,
    own_buf,
    kv_buf,
    code_buf,
    gate_buf,
    out_buf,
    misc_sem,
):
    rows, local_w = own_buf.shape
    per_chunk = order.shape[0] // chunks
    patch_tok = rows // per_chunk
    age = 2 * scalars[0] + parity - scalars[1]
    chunk = lax.div(age, 2)
    active = (age >= 0) & (lax.rem(age, 2) == 0) & (chunk < chunks)

    @pl.when(active)
    def _():
        patch_rows = []
        for i in range(per_chunk):
            patch = order[chunk * per_chunk + i]
            patch_rows.append(pl.ds(pl.multiple_of(patch * patch_tok, patch_tok), patch_tok))
        loads = [
            pltpu.make_async_copy(fresh, projected, misc_sem.at[0]),
            pltpu.make_async_copy(own_rows, own_buf, misc_sem.at[1]),
            pltpu.make_async_copy(gate_row, gate_buf, misc_sem.at[2]),
        ]
        for i in range(per_chunk):
            loads.append(pltpu.make_async_copy(kv_before, kv_buf.at[i], misc_sem.at[3 + i]))
            loads.append(
                pltpu.make_async_copy(
                    chosen.at[patch_rows[i]], code_buf.at[i], misc_sem.at[3 + per_chunk + i]
                )
            )
        for copy in loads:
            copy.start()
        for copy in loads:
            copy.wait()

        gate = gate_buf[...]
        nt = (((1,), (1,)), ((), ()))
        heads = local_w // HEAD_DIM
        chunk_at = [pl.ds(i * patch_tok, patch_tok) for i in range(per_chunk)]
        head_at = [pl.ds(head * HEAD_DIM, HEAD_DIM) for head in range(heads)]
        backs = []
        chances = []
        for i in range(per_chunk):
            for j in range(i + 1):
                for part in range(2):
                    kv_buf[i, part, patch_rows[j], :] = projected[1 + part, chunk_at[j], :]
        for i in range(per_chunk):
            for part in range(2):
                backs.append(
                    pltpu.make_async_copy(
                        projected.at[1 + part, chunk_at[i]],
                        kv.at[part, patch_rows[i]],
                        misc_sem.at[3 + 2 * per_chunk + 2 * i + part],
                    )
                )
                backs[-1].start()
            scores = jnp.concatenate(
                [
                    lax.dot_general(
                        projected[0, chunk_at[i], cols],
                        kv_buf[i, 0, :, cols],
                        nt,
                        preferred_element_type=jnp.float32,
                    )
                    for cols in head_at
                ],
                axis=0,
            )
            attended = jnp.concatenate([code_buf[i] > 0.5] * heads, axis=0)
            scores = jnp.where(attended, scores * HEAD_DIM ** (-0.5), MASKED)
            largest = jnp.max(scores, axis=-1, keepdims=True)
            raised = jnp.exp(scores - largest)
            total = jnp.sum(raised, axis=-1, keepdims=True)
            chances.append((raised * (1.0 / total)).astype(jnp.bfloat16))
        for i in range(per_chunk):
            for head, cols in enumerate(head_at):
                mixed = jnp.dot(
                    chances[i][head * patch_tok : (head + 1) * patch_tok],
                    kv_buf[i, 1, :, cols],
                    preferred_element_type=jnp.float32,
                )
                mixed = mixed.astype(jnp.bfloat16).astype(jnp.float32)
                own = own_buf[chunk_at[i], cols].astype(jnp.float32)
                gate_part = gate[:, head * HEAD_DIM : (head + 1) * HEAD_DIM]
                out_buf[chunk_at[i], cols] = (own + gate_part * mixed).astype(jnp.bfloat16)
        backs.append(pltpu.make_async_copy(out_buf, out, misc_sem.at[0]))
        backs[-1].start()
        for i in range(per_chunk):
            backs.append(
                pltpu.make_async_copy(
                    out_buf.at[pl.ds(i * patch_tok, patch_tok)],
                    results.at[patch_rows[i]],
                    misc_sem.at[3 + i],
                )
            )
            backs[-1].start()
        for copy in backs:
            copy.wait()


def keep_in_vmem(parity, scalars, value, after):
    def body(scalars, src, after, dst, sem):
        @pl.when(lax.rem(scalars[1], 2) == parity)
        def _():
            copy = pltpu.make_async_copy(src, dst, sem)
            copy.start()
            copy.wait()

    any_spec = pl.BlockSpec(memory_space=pl.ANY)
    return pl.pallas_call(
        body,
        out_shape=pltpu.VMEM(value.shape, value.dtype),
        in_specs=[pl.BlockSpec(memory_space=pltpu.SMEM), any_spec, any_spec],
        out_specs=any_spec,
        scratch_shapes=[pltpu.SemaphoreType.DMA(())],
        compiler_params=pltpu.CompilerParams(vmem_limit_bytes=1024 * 1024),
        name="keep",
    )(scalars, value, after)


def run_attend(parity, chunks, scalars, order, fresh, own, chosen, gate, kv, results):
    per_chunk = order.shape[0] // chunks
    any_spec = pl.BlockSpec(memory_space=pl.ANY)
    smem_spec = pl.BlockSpec(memory_space=pltpu.SMEM)
    return pl.pallas_call(
        functools.partial(attend_kernel, parity, chunks),
        out_shape=(
            jax.ShapeDtypeStruct(own.shape, jnp.bfloat16),
            jax.ShapeDtypeStruct(kv.shape, kv.dtype),
            jax.ShapeDtypeStruct(results.shape, results.dtype),
        ),
        in_specs=[smem_spec] * 2 + [any_spec] * 6,
        out_specs=(any_spec,) * 3,
        scratch_shapes=[
            pltpu.VMEM(fresh.shape, jnp.bfloat16),
            pltpu.VMEM(own.shape, jnp.bfloat16),
            pltpu.VMEM((per_chunk, *kv.shape), jnp.bfloat16),
            pltpu.VMEM((per_chunk, own.shape[0] // per_chunk, chosen.shape[1]), jnp.float32),
            pltpu.VMEM(gate.shape, jnp.float32),
            pltpu.VMEM(own.shape, jnp.bfloat16),
            pltpu.SemaphoreType.DMA((3 + 4 * per_chunk,)),
        ],
        input_output_aliases={6: 1, 7: 2},
        compiler_params=pltpu.CompilerParams(vmem_limit_bytes=12 * 1024 * 1024),
        name="attend",
    )(scalars, order, fresh, own, chosen, gate, kv, results)


def normalize(rows, shift_row, scale_row):
    floated = rows.astype(jnp.float32)
    average = jnp.mean(floated, axis=-1, keepdims=True)
    centred = floated - average
    spread = jnp.mean(centred * centred, axis=-1, keepdims=True)
    return (centred * lax.rsqrt(spread + epsilon) * (1.0 + scale_row) + shift_row).astype(
        jnp.bfloat16
    )


def pair_list(pipe_count, seq_count, parity, by):
    return [
        (s * seq_count + q, (s + 1) * seq_count + (q + by) % seq_count)
        for s in range(parity, pipe_count - 1, 2)
        for q in range(seq_count)
    ]


def chosen_keys(tiles, tile_len):
    n_tiles = tiles.shape[0]
    tile_ids = jnp.arange(n_tiles, dtype=jnp.int32)
    chosen = jnp.any(tiles[:, :, None] == tile_ids[None, None, :], axis=1).astype(jnp.float32)
    return jnp.repeat(jnp.repeat(chosen, tile_len, 0), tile_len, 1)


def local(latent, w_qkv, modulation, timestep, order, tiles, stale_kv):
    patches, rows_dev, width = latent.shape
    local_w = w_qkv.shape[3]
    seq_count = lax.axis_size("seq")
    pipe_count = lax.axis_size("pipe")
    section_rank = lax.axis_index("pipe").astype(jnp.int32)
    seq_rank = lax.axis_index("seq").astype(jnp.int32)
    patch_tok = rows_dev * seq_count
    rows = patches * patch_tok
    chunk_rows = rows // CHUNKS
    weights = jnp.transpose(w_qkv[0], (1, 0, 2))
    mod_rows = lax.dynamic_index_in_dim(modulation[0], timestep[0], 0, keepdims=False)
    gate = lax.dynamic_slice_in_dim(mod_rows[2:], seq_rank * local_w, local_w, 1)
    kv = jnp.moveaxis(stale_kv[0], 2, 0).reshape(2, rows, local_w)
    chosen = chosen_keys(tiles, patch_tok // TILES_P)

    quarters = [latent] + [
        lax.ppermute(
            latent, ("pipe", "seq"), [(q, (q + by) % seq_count) for q in range(seq_count)]
        )
        for by in range(1, seq_count)
    ]
    tokens = jnp.stack(
        [lax.select_n((seq_rank + seq_count - j) % seq_count, *quarters) for j in range(seq_count)],
        axis=1,
    ).reshape(patches, patch_tok, width)[order]
    tokens = tokens.reshape(CHUNKS, chunk_rows, width)

    def send(out, parity):
        arrived = [None] * seq_count
        for by in SEND_ORDER:
            arrived[by] = lax.ppermute(
                out, ("pipe", "seq"), pair_list(pipe_count, seq_count, parity, by)
            )
        return tuple(arrived)

    def two_turns(i, carry):
        out, kv, results = carry
        scalars = jnp.stack([i, section_rank, seq_rank])
        for parity in range(2):
            pieces = send(out, 1 - parity)
            held = keep_in_vmem(parity, scalars, weights, out)
            whole = jnp.concatenate(
                [lax.select_n((seq_rank + seq_count - j) % seq_count, *pieces) for j in range(seq_count)],
                axis=1,
            )
            own = pieces[0]
            if parity == 0:
                chunk = jnp.clip(i, 0, CHUNKS - 1)
                entry = lax.dynamic_index_in_dim(tokens, chunk, 0, keepdims=False)
                whole = jnp.where(section_rank == 0, entry, whole)
                entry = lax.dynamic_slice(
                    tokens, (chunk, 0, seq_rank * local_w), (1, chunk_rows, local_w)
                )[0]
                own = jnp.where(section_rank == 0, entry, own)
            normed = normalize(whole, mod_rows[0], mod_rows[1])
            fresh = lax.dot_general(
                normed, held, (((1,), (1,)), ((), ())), preferred_element_type=jnp.float32
            ).astype(jnp.bfloat16)
            fresh = jnp.moveaxis(fresh, 1, 0)
            out, kv, results = run_attend(
                parity, CHUNKS, scalars, order, fresh, own, chosen, gate, kv, results
            )
        return out, kv, results

    turns = pipe_count + 2 * (CHUNKS - 1)
    _, kv, results = lax.fori_loop(
        0,
        (turns + 1) // 2,
        two_turns,
        (
            jnp.zeros((chunk_rows, local_w), jnp.bfloat16),
            kv,
            jnp.zeros((rows, local_w), jnp.bfloat16),
        ),
    )
    columns = results.reshape(patches, seq_count, rows_dev, local_w)
    parts = []
    for by in range(seq_count):
        target = (seq_rank + by) % seq_count
        part = lax.dynamic_index_in_dim(columns, target, 1, keepdims=False)
        if by:
            pairs = [
                (s * seq_count + q, s * seq_count + (q + by) % seq_count)
                for s in range(pipe_count)
                for q in range(seq_count)
            ]
            part = lax.ppermute(part, ("pipe", "seq"), pairs)
        parts.append(part)
    finished = jnp.concatenate(
        [lax.select_n((seq_rank + seq_count - j) % seq_count, *parts) for j in range(seq_count)],
        axis=2,
    )
    return finished[None]


def solution(mesh):
    return jax.shard_map(
        local,
        mesh=mesh,
        in_specs=(
            P("batch", "seq", None),
            P("pipe", None, None, "seq"),
            P("pipe", None, None, None),
            P(),
            P("batch"),
            P("batch", None),
            P("pipe", "batch", None, None, "seq"),
        ),
        out_specs=P("pipe", "batch", "seq", None),
        check_vma=False,
    )
```
